32 devices in a mesh: outer: 4 (over y, x), inner: 8 (over z, core).
Axes of the slice: x: 2, y: 2, z: 4, core: 2. Of those that a mesh axis runs over, the one named last changes fastest.
Arguments:
- queries: bfloat16 [8192, 1024], P(('outer', 'inner')), may hold values from -6 to 6
- keys: bfloat16 [2, 8192, 1024], P(None, ('outer', 'inner')), may hold values from -6 to 6
- values: bfloat16 [2, 8192, 1024], P(None, ('outer', 'inner')), may hold values from -6 to 6
- betas: float32 [2, 8, 8192], P(None, None, ('outer', 'inner')), may hold values from 0 to 2
- log_decay: float32 [8, 8192], P(None, ('outer', 'inner')), may hold values from -1 to 0
- out_gain: float32 [128], replicated, may hold values from 0.5 to 1.5
Outputs:
- mixed: bfloat16 [8192, 1024], P(('outer', 'inner'))
The draws below stay inside these ranges and needn't reach their ends.
All inputs are finite; a program needn't handle non-finite values.
Results may differ from the reference program's by a relative error of at most 0.0018.
Values sent between devices are 32-bit elements; how exact they have to be, the bound alone decides.
A program may use at most 128 MiB of HBM per device.

```python
import jax
import jax.numpy as jnp
from jax import lax

HEADS = 8
DK = 128
DV = 128
BLOCK_LEN = 64
TOK_DEV = 256
TOKENS = 8192


def head_speed(key):
    order = jax.random.permutation(jax.random.fold_in(key, 101), HEADS)
    quick_count = max(1, HEADS // 2)
    quick = (order < quick_count).astype(jnp.float32)
    device_log = jax.random.uniform(jax.random.fold_in(key, 102), (TOKENS // TOK_DEV,), jnp.float32, jnp.log(0.5), jnp.log(2.0))
    device_factor = jnp.repeat(jnp.exp(device_log), TOK_DEV)
    return (quick, device_factor)


def draw_log_decay(key, part):
    quick, device_factor = head_speed(key)
    quick_rate = jnp.exp(jax.random.uniform(jax.random.fold_in(key, 201), (HEADS, 1), jnp.float32, jnp.log(1.0 / 50.0), jnp.log(1.0 / 30.0)))
    slow_rate = jnp.exp(jax.random.uniform(jax.random.fold_in(key, 202), (HEADS, 1), jnp.float32, jnp.log(0.1), jnp.log(0.4))) / TOKENS
    rate = jnp.where(quick[:, None] > 0.5, quick_rate, slow_rate)
    rough = jax.random.uniform(jax.random.fold_in(key, 203), (HEADS, TOKENS), jnp.float32, 0.5, 1.5)
    base_log = -rate * rough * device_factor[None, :]
    places = jax.random.randint(jax.random.fold_in(key, 204), (2,), 0, TOKENS)
    position = jnp.arange(TOKENS, dtype=jnp.int32)
    struck = jnp.max((position[None, :] == places[:, None]).astype(jnp.float32), 0)
    depth = jax.random.uniform(jax.random.fold_in(key, 205), (HEADS, TOKENS), jnp.float32, jnp.log(0.55), jnp.log(0.8))
    return base_log + struck[None, :] * depth


def draw_betas(key, part):
    quick, device_factor = head_speed(key)
    normal_part = jnp.clip(jax.random.normal(jax.random.fold_in(key, 301), (2, HEADS, TOKENS), jnp.float32), -4.0, 4.0)
    quick_beta = 2.0 * jax.nn.sigmoid(1.2 * normal_part)
    slow_gap = 40.0 / TOKENS * jax.random.uniform(jax.random.fold_in(key, 303), (2, HEADS, TOKENS), jnp.float32, 0.5, 1.5) * device_factor[None, None, :]
    slow_beta = 2.0 - slow_gap
    return jnp.where(quick[None, :, None] > 0.5, quick_beta, slow_beta)


def level_of(own_key, dims, cuts, low, top_value):
    level, own = 1.0, jax.random.fold_in(own_key, 6)
    for dim, parts in cuts:
        draws = jnp.exp(jax.random.uniform(jax.random.fold_in(own, dim), (parts,), jnp.float32, low / len(cuts), top_value / len(cuts)))
        level = level * jnp.repeat(draws, dims[dim] // parts).reshape([-1 if axis == dim else 1 for axis in range(len(dims))])
    return level


def centred(key, dims, scale, limit, cuts=(), held_as=jnp.bfloat16):
    values = scale * jax.random.normal(key, dims, jnp.float32)
    if cuts:
        values = values * level_of(key, dims, cuts, -0.22, 0.18)
    return jnp.clip(values, -limit, limit).astype(held_as)


def setup_inputs(seed: int = 0) -> dict:
    key_list = jax.random.split(jax.random.key(seed), 7)
    return {
        "queries": centred(key_list[0], (TOKENS, HEADS * DK), 1.0, 6.0, ((0, 32),)),
        "keys": centred(key_list[1], (2, TOKENS, HEADS * DK), 1.0, 6.0, ((1, 32),)),
        "values": centred(key_list[2], (2, TOKENS, HEADS * DV), 1.0, 6.0, ((1, 32),)),
        "betas": draw_betas(jax.random.fold_in(key_list[6], 71), 0),
        "log_decay": draw_log_decay(jax.random.fold_in(key_list[6], 71), 0),
        "out_gain": jnp.clip(1.0 + 0.1 * jax.random.normal(key_list[5], (DV,), jnp.float32), 0.5, 1.5),
    }


HIGHEST = lax.Precision.HIGHEST

def prepare(queries, keys, values, betas, log_decay):
    length = queries.shape[0]
    heads = betas.shape[1]
    width_k = queries.shape[1] // heads
    width_v = values.shape[2] // heads
    blocks = length // BLOCK_LEN
    reflect = 2 * BLOCK_LEN
    query_f = queries.astype(jnp.float32).reshape(blocks, BLOCK_LEN, heads, width_k).transpose(0, 2, 1, 3)
    query_inv = lax.rsqrt(lax.optimization_barrier(jnp.sum(query_f * query_f, -1)) + 1e-06)
    query_n = query_f * query_inv[..., None]
    key_f = keys.astype(jnp.float32).reshape(2, blocks, BLOCK_LEN, heads, width_k).transpose(1, 3, 2, 0, 4)
    key_f = key_f.reshape(blocks, heads, reflect, width_k)
    key_inv = lax.rsqrt(lax.optimization_barrier(jnp.sum(key_f * key_f, -1)) + 1e-06)
    key_n = key_f * key_inv[..., None]
    value_n = values.astype(jnp.float32).reshape(2, blocks, BLOCK_LEN, heads, width_v).transpose(1, 3, 2, 0, 4)
    value_n = value_n.reshape(blocks, heads, reflect, width_v)
    beta_r = betas.reshape(2, heads, blocks, BLOCK_LEN).transpose(2, 1, 3, 0).reshape(blocks, heads, reflect)
    decay_t = log_decay.reshape(heads, blocks, BLOCK_LEN).transpose(1, 0, 2)
    decay_r = jnp.stack([decay_t, jnp.zeros_like(decay_t)], -1).reshape(blocks, heads, reflect)
    cumulative = jnp.cumsum(decay_r, -1)
    row_idx = lax.broadcasted_iota(jnp.int32, (reflect, reflect), 0)
    col_idx = lax.broadcasted_iota(jnp.int32, (reflect, reflect), 1)
    key_gram = jnp.einsum('nhrd,nhsd->nhrs', key_f, key_f, precision=HIGHEST) * key_inv[..., :, None] * key_inv[..., None, :]
    fall_off = jnp.exp(jnp.minimum(cumulative[..., :, None] - cumulative[..., None, :], 0.0))
    strict_low = jnp.where(row_idx > col_idx, key_gram * fall_off, 0.0)
    system = jnp.eye(reflect, dtype=jnp.float32) + beta_r[..., :, None] * strict_low
    scaled = jnp.exp(cumulative)
    right_side = jnp.concatenate([(beta_r * scaled)[..., None] * key_n, beta_r[..., None] * value_n], -1)
    solved = lax.linalg.triangular_solve(system, right_side, left_side=True, lower=True, unit_diagonal=True)
    write_key = solved[..., :width_k]
    write_val = solved[..., width_k:]
    tok_idx = lax.broadcasted_iota(jnp.int32, (BLOCK_LEN, reflect), 0)
    ref_idx = lax.broadcasted_iota(jnp.int32, (BLOCK_LEN, reflect), 1)
    query_cum = cumulative.reshape(blocks, heads, BLOCK_LEN, 2)[..., 1]
    query_key = jnp.einsum('nhcd,nhsd->nhcs', query_f, key_f, precision=HIGHEST) * query_inv[..., :, None] * key_inv[..., None, :]
    fade = jnp.exp(jnp.minimum(query_cum[..., :, None] - cumulative[..., None, :], 0.0))
    reach = jnp.where(ref_idx <= 2 * tok_idx + 1, query_key * fade, 0.0)
    reduced = jnp.exp(query_cum)[..., None] * query_n - jnp.einsum('nhcs,nhsd->nhcd', reach, write_key, precision=HIGHEST)
    local_out = jnp.einsum('nhcs,nhsd->nhcd', reach, write_val, precision=HIGHEST)
    last_cum = cumulative[..., -1:]
    tail = jnp.exp(last_cum - cumulative)
    trans = jnp.exp(last_cum)[..., None] * jnp.eye(width_k, dtype=jnp.float32)
    trans = trans - jnp.einsum('nhsd,nhse->nhde', tail[..., None] * write_key, key_n, precision=HIGHEST)
    inject = jnp.einsum('nhsd,nhse->nhde', tail[..., None] * write_val, key_n, precision=HIGHEST)
    return (reduced, local_out, trans, inject)

def finish(readout, out_gain):
    mean_sq = lax.optimization_barrier(jnp.mean(readout * readout, -1, keepdims=True))
    normed = readout * lax.rsqrt(mean_sq + 1e-05) * out_gain
    blocks, heads, span, width_v = normed.shape
    return normed.transpose(0, 2, 1, 3).reshape(blocks * span, heads * width_v).astype(jnp.bfloat16)

def reference(queries, keys, values, betas, log_decay, out_gain):
    groups = TOKENS // TOK_DEV
    query_g = queries.reshape(groups, TOK_DEV, HEADS * DK)
    key_g = keys.reshape(2, groups, TOK_DEV, HEADS * DK).transpose(1, 0, 2, 3)
    value_g = values.reshape(2, groups, TOK_DEV, HEADS * DV).transpose(1, 0, 2, 3)
    beta_g = betas.reshape(2, HEADS, groups, TOK_DEV).transpose(2, 0, 1, 3)
    decay_g = log_decay.reshape(HEADS, groups, TOK_DEV).transpose(1, 0, 2)

    def group_step(state, inputs):
        reduced, local_out, trans, inject = prepare(*inputs)

        def block_step(inner_state, pieces):
            red_b, loc_b, trans_b, inj_b = pieces
            readout = jnp.einsum('hcd,hed->hce', red_b, inner_state, precision=HIGHEST) + loc_b
            next_state = jnp.einsum('hde,hef->hdf', inner_state, trans_b, precision=HIGHEST) + inj_b
            return (next_state, readout)
        state, readouts = lax.scan(block_step, state, (reduced, local_out, trans, inject))
        return (state, finish(readouts, out_gain))
    start = jnp.zeros((HEADS, DV, DK), jnp.float32)
    final_state, outputs = lax.scan(group_step, start, (query_g, key_g, value_g, beta_g, decay_g))
    return outputs.reshape(TOKENS, HEADS * DV)
```

```python
import functools

import jax
import jax.numpy as jnp
from jax import lax
from jax.experimental import pallas as pl
from jax.experimental.pallas import tpu as pltpu
from jax.sharding import PartitionSpec as P

BLOCK_LEN = 64
F32 = jnp.float32
BF16 = jnp.bfloat16


def split(x):
    high = x.astype(BF16)
    low = (x - high.astype(F32)).astype(BF16)
    return high, low


def dot(a, b):
    return lax.dot_general(a, b, (((1,), (0,)), ((), ())), preferred_element_type=F32)


def dot_t(a, b):
    return lax.dot_general(a, b, (((1,), (1,)), ((), ())), preferred_element_type=F32)


def wide(x):
    return jnp.concatenate(split(x), 1)


def mul(a, b):
    a2 = wide(a)
    bh, bl = split(b)
    if b.shape[1] == 128:
        row = jnp.concatenate([bh, bl], 1)
        both = dot(a2, jnp.concatenate([row, row], 0))
        return both[:, :128] + both[:, 128:]
    return dot(a2, jnp.concatenate([bh, bh], 0)) + dot(a2[:, :128], bl)


def add_right(x, y):
    return jnp.concatenate([x[:, :128], x[:, 128:] + y], 1)


def apply3(a, b):
    ah, al = split(a)
    bh, bl = split(b)
    return dot(jnp.concatenate([ah, al], 1), jnp.concatenate([bh, bh], 0)) + dot(ah, bl)


def gathered_rows(decay, beta0, beta1):
    lane = lax.broadcasted_iota(jnp.int32, decay.shape[:1] + (128,), 1)
    group = lane >> 4
    out = []
    for half in range(decay.shape[1] // 128):
        at = slice(128 * half, 128 * half + 128)
        c, b0, b1 = decay[:, at], beta0[:, at], beta1[:, at]
        width = 1
        while width < BLOCK_LEN:
            c = c + jnp.where((lane & (BLOCK_LEN - 1)) >= width, pltpu.roll(c, width, 1), 0.0)
            width *= 2
        for first in (0, BLOCK_LEN):

            def moved(x, step):
                shift = (16 * step - first) % 128
                return pltpu.roll(x, shift, 1) if shift else x

            c_row = moved(c, 0)
            beta_row = moved(b0, 0)
            for g in range(1, 8):
                step = g // 2 + g % 2
                c_row = jnp.where(group == g, moved(c, step), c_row)
                beta_row = jnp.where(group == g, moved(b1 if g % 2 else b0, step), beta_row)
            out.append((c_row, beta_row))
    return out


def mixed_rows(x0, x1):
    parts = []
    for at in range(0, BLOCK_LEN, 16):
        parts += [x0[at : at + 16], x1[at : at + 16]]
    return jnp.concatenate(parts, 0)


def rank_of(x):
    return 2 * (16 * (x >> 5) + (x & 15)) + ((x >> 4) & 1)


def product3(ah, al, bh, bl):
    rows = ah.shape[0]
    o = dot(jnp.concatenate([ah, al], 0), jnp.concatenate([bh, bl], 1))
    return o[:rows, :128] + (o[:rows, 128:] + (o[rows:, :128] + o[rows:, 128:]))


def head_maps(blocks, heads_in, load, emit, middle=None):
    span = BLOCK_LEN
    size = 2 * span
    row = lax.broadcasted_iota(jnp.int32, (size, size), 0)
    col = lax.broadcasted_iota(jnp.int32, (size, size), 1)
    eye = row == col
    eye_f = eye.astype(F32)
    lower = (rank_of(row) > rank_of(col)).astype(F32)
    token = rank_of(col) >> 1
    seen = (token[:span] <= row[:span]).astype(F32)
    own = (token[:span] == row[:span]) & ((col[:span] & 16) == 0)
    row_c, col_c = row[:32], col[:32] & 31
    rank_r, rank_c = rank_of(row_c), rank_of(col_c)
    differ = rank_r ^ rank_c
    eye_c = (row_c == col_c).astype(F32)
    levels = []
    for width in (1, 2, 4, 8, 16):
        levels.append(((differ >= width) & (differ < 2 * width) & (rank_r > rank_c)).astype(BF16))
    part = (col >> 5)[:32]
    chunk = [part == c for c in range(4)]
    zero_c = jnp.zeros((32, 128), BF16)

    def spread(x):
        return jnp.concatenate([jnp.where(chunk[c], x, zero_c) for c in range(4)], 0)

    def diagonal(x):
        y = jnp.where(chunk[0], x[:32], x[32:64])
        y = jnp.where(chunk[2], x[64:96], y)
        return jnp.where(chunk[3], x[96:], y)

    def below(x):
        return jnp.where(chunk[0], x[32:64], jnp.where(chunk[2], x[96:], zero_c))

    work = []
    for i, n in [(i, n) for i in range(heads_in) for n in range(blocks)]:
        q_b, k_b, v_b, c_row, beta_row = load(i, n)
        both = dot_t(jnp.concatenate([k_b, q_b], 0), k_b)
        gram, cross = both[:size], both[size:]
        q_f = q_b.astype(F32)
        ki_row = lax.rsqrt(jnp.sum(jnp.where(eye, gram, 0.0), 0, keepdims=True) + 1e-06)
        qi_col = lax.rsqrt(jnp.sum(q_f * q_f, 1, keepdims=True) + 1e-06)
        up = jnp.exp(c_row)
        key_row = beta_row * ki_row * up
        away_row = ki_row * jnp.exp(-c_row)
        last = c_row[:, size - 1 :]
        tail_row = ki_row * jnp.exp(last - c_row)
        key_col = jnp.sum(jnp.where(eye, key_row, 0.0), 1, keepdims=True)
        query_col = qi_col * jnp.sum(jnp.where(own, up, 0.0), 1, keepdims=True)
        low_h, low_l = split(gram * key_col * away_row * lower)
        reach = cross * query_col * away_row * seen
        query = q_f * query_col
        k_t = jnp.transpose(k_b.astype(F32)) * tail_row
        work.append(dict(k=k_b, v=v_b, beta=beta_row, key=key_row, last=jnp.exp(last), low_h=low_h, low_l=low_l,
                         left=jnp.concatenate([reach, k_t], 0), query=query))

    for w in work:
        w["dh"], w["dl"] = diagonal(w["low_h"]), diagonal(w["low_l"])
        first = (w["dh"] * levels[0]).astype(F32) + (w["dl"] * levels[0]).astype(F32)
        w["t"] = eye_c - first
    for mask in levels[1:]:
        for w in work:
            w["th"], w["tl"] = split(w["t"])
            w["p"] = product3(w["dh"] * mask, w["dl"] * mask, spread(w["th"]), spread(w["tl"]))
        for w in work:
            ph, pl_ = split(w["p"])
            w["t"] = w["t"] - product3(w["th"], w["tl"], spread(ph), spread(pl_))
    if middle is not None:
        middle()
    for w in work:
        w["th"], w["tl"] = split(w["t"])
        w["p"] = product3(below(w["low_h"]), below(w["low_l"]), spread(w["th"]), spread(w["tl"]))
    for w in work:
        ph, pl_ = split(w["p"])
        rh, rl = split(pltpu.roll(w["t"], 96, 1))
        w["p"] = product3(rh, rl, spread(ph), spread(pl_))
    for w in work:
        t, p = w["t"], w["p"]
        w["ta"] = jnp.concatenate(
            [jnp.where(chunk[0], t, 0.0), jnp.where(chunk[1], t, jnp.where(chunk[0], -p, 0.0))], 0
        )
        w["tb"] = jnp.concatenate(
            [jnp.where(chunk[2], t, 0.0), jnp.where(chunk[3], t, jnp.where(chunk[2], -p, 0.0))], 0
        )
        ah, al = split(w["ta"])
        w["p"] = product3(w["low_h"][span:, :span], w["low_l"][span:, :span], ah, al)
    zero_s = jnp.zeros((span, size), BF16)
    for w in work:
        ph, pl_ = split(w["p"])
        bh, bl = split(w["tb"])
        w["tb"] = w["tb"] - product3(
            bh, bl, jnp.concatenate([zero_s, ph], 0), jnp.concatenate([zero_s, pl_], 0)
        )

    for w in work:
        t = jnp.concatenate([w["ta"], w["tb"]], 0)
        k2 = jnp.concatenate([w["k"], w["k"]], 0)
        v2 = jnp.concatenate([w["v"], w["v"]], 0)
        w["written"] = jnp.concatenate([dot(wide(t * w["key"]), k2), dot(wide(t * w["beta"]), v2)], 1)
    for w in work:
        got = apply3(w["left"], w["written"])
        read = jnp.concatenate([w["query"] - got[:span, :128], got[:span, 128:]], 1)
        trans = w["last"] * eye_f - got[span:, :128]
        w["rows"] = jnp.concatenate([read, jnp.concatenate([trans, got[span:, 128:]], 1)], 0)

    level = [[work[i * blocks + n]["rows"] for n in range(blocks)] for i in range(heads_in)]
    level = [[[x[:span], x[span:]] for x in parts] for parts in level]
    while len(level[0]) > 1:
        merged = []
        for parts in level:
            pairs = []
            for first, later in zip(parts[::2], parts[1::2]):
                moved = jnp.concatenate(later, 0)
                moved = add_right(apply3(moved[:, :128], first[-1]), moved[:, 128:])
                cut = span * (len(later) - 1)
                pairs.append(first[:-1] + [moved[span * j : span * (j + 1)] for j in range(len(later) - 1)] + [moved[cut:]])
            merged.append(pairs)
        level = merged
    states = []
    for i in range(heads_in):
        parts = level[i][0]
        for n in range(blocks):
            emit(i, n, parts[n][:, :128], parts[n][:, 128:])
        states.append(parts[-1])
    return states


def local_kernel(blocks, q_ref, k_ref, v_ref, s_ref, x_ref, c_ref, b_ref):
    def load(i, n):
        at = pl.ds(n * BLOCK_LEN, BLOCK_LEN)
        k_b = mixed_rows(k_ref[0, at, :], k_ref[1, at, :])
        v_b = mixed_rows(v_ref[0, at, :], v_ref[1, at, :])
        return q_ref[at, :], k_b, v_b, s_ref[0, n : n + 1, :], s_ref[0, blocks + n : blocks + n + 1, :]

    def emit(i, n, carried, base):
        at = pl.ds(n * BLOCK_LEN, BLOCK_LEN)
        c_ref[0, at, :] = carried
        b_ref[0, at, :] = base

    x_ref[0] = head_maps(blocks, 1, load, emit)[0]


def small_rows(betas, log_decay):
    heads, length = log_decay.shape
    blocks = length // BLOCK_LEN
    beta = betas.reshape(2, heads, blocks, BLOCK_LEN // 16, 16).transpose(1, 2, 3, 0, 4)
    beta = beta.reshape(heads, blocks, 2 * BLOCK_LEN)
    decay = jnp.cumsum(log_decay.reshape(heads, blocks, BLOCK_LEN), -1)
    decay = decay.reshape(heads, blocks, BLOCK_LEN // 16, 1, 16)
    decay = jnp.concatenate([decay, decay], 3).reshape(heads, blocks, 2 * BLOCK_LEN)
    return jnp.concatenate([decay, beta], 1)


def local_phase(queries, keys, values, betas, log_decay):
    length = queries.shape[0]
    heads = betas.shape[1]
    blocks = length // BLOCK_LEN
    small = small_rows(betas, log_decay)
    return pl.pallas_call(
        functools.partial(local_kernel, blocks),
        grid=(heads,),
        in_specs=[
            pl.BlockSpec((length, 128), lambda h: (0, h)),
            pl.BlockSpec((2, length, 128), lambda h: (0, 0, h)),
            pl.BlockSpec((2, length, 128), lambda h: (0, 0, h)),
            pl.BlockSpec((1, 2 * blocks, 128), lambda h: (h, 0, 0)),
        ],
        out_specs=[
            pl.BlockSpec((1, 128, 256), lambda h: (h, 0, 0)),
            pl.BlockSpec((1, length, 128), lambda h: (h, 0, 0)),
            pl.BlockSpec((1, length, 128), lambda h: (h, 0, 0)),
        ],
        out_shape=[
            jax.ShapeDtypeStruct((heads, 128, 256), F32),
            jax.ShapeDtypeStruct((heads, length, 128), F32),
            jax.ShapeDtypeStruct((heads, length, 128), F32),
        ],
        name="local_phase",
    )(queries, keys, values, small)


def then(earlier, later):
    return add_right(mul(later[:, :128], earlier), later[:, 128:])


def normed(carried, base, state, gain):
    readout = mul(carried, state) + base
    mean_sq = jnp.mean(readout * readout, 1, keepdims=True)
    return (readout * lax.rsqrt(mean_sq + 1e-05) * gain).astype(BF16)


def whole_kernel(
    inner, outer, q_ref, k_ref, v_ref, beta_ref, decay_ref, g_ref, o_ref,
    away, near, own, even_map, sent, got, groups, mine, ready, came, aside, beside, c_buf, b_buf, rows,
    send0, recv0, send1, recv1, send2, recv2, send3, recv3, send4, recv4,
):
    mesh_id = pl.DeviceIdType.MESH
    length = q_ref.shape[0]
    blocks = length // BLOCK_LEN
    me = lax.axis_index("inner")
    group = lax.axis_index("outer")
    core, chip, chips = me % 2, me // 2, inner // 2
    partner = chip * 2 + 1 - core
    groups[...] = jnp.zeros_like(groups)
    barrier = pltpu.get_barrier_semaphore()
    for d in range(1, chips):
        pl.semaphore_signal(
            barrier, inc=1, device_id=(group, (chip + d) % chips * 2 + core), device_id_type=mesh_id
        )
    pl.semaphore_signal(barrier, inc=1, device_id=(group, partner), device_id_type=mesh_id)
    for d in range(1, outer):
        pl.semaphore_signal(barrier, inc=1, device_id=((group + d) % outer, me), device_id_type=mesh_id)
    for n, (c_row, beta_row) in enumerate(gathered_rows(decay_ref[...], beta_ref[0], beta_ref[1])):
        rows[n] = c_row
        rows[blocks + n] = beta_row

    def apart(turn):
        return chips // 2 + (turn + 1) // 2 * (1 - 2 * (turn % 2))

    def near_copy(turn):
        return pltpu.make_async_remote_copy(
            src_ref=away.at[turn], dst_ref=near.at[turn],
            send_sem=send0.at[turn], recv_sem=recv0.at[turn],
            device_id=(group, partner), device_id_type=mesh_id,
        )

    def map_copy(d):
        return pltpu.make_async_remote_copy(
            src_ref=sent.at[d], dst_ref=got.at[d],
            send_sem=send1.at[d], recv_sem=recv1.at[d],
            device_id=(group, (chip + d) % chips * 2 + core), device_id_type=mesh_id,
        )

    def chip_map(turn):
        near_copy(turn).wait()
        here, there = own[turn], near[turn]
        even = jnp.where(core == 0, here, there)
        odd = jnp.where(core == 0, there, here)
        even_map[apart(turn)] = even
        return then(even, odd)

    def step(turn, carry):
        far = (chip + apart(turn)) % chips * 2
        heads = [far + core, far + 1 - core]

        def load(i, n):
            at = pl.ds(n * BLOCK_LEN, BLOCK_LEN)
            lanes = pl.ds(pl.multiple_of(heads[i] * 128, 128), 128)
            k_b = mixed_rows(k_ref[0, at, lanes], k_ref[1, at, lanes])
            v_b = mixed_rows(v_ref[0, at, lanes], v_ref[1, at, lanes])
            one = pl.ds(heads[i], 1)
            return q_ref[at, lanes], k_b, v_b, rows[n, one, :], rows[blocks + n, one, :]

        def emit(i, n, carried, base):
            at = pl.ds(n * BLOCK_LEN, BLOCK_LEN)
            c_buf[heads[i], at, :] = carried
            b_buf[heads[i], at, :] = base

        def middle():
            @pl.when(turn == 0)
            def _():
                pl.semaphore_wait(barrier, chips + outer - 1)

            @pl.when(turn > 0)
            def _():
                to = apart(turn - 1)
                sent[to] = chip_map(turn - 1)
                map_copy(to).start()

        states = head_maps(blocks, 2, load, emit, middle)

        away[turn] = states[1]
        near_copy(turn).start()
        own[turn] = states[0]
        return carry

    lax.fori_loop(0, chips, step, 0)
    got[0] = chip_map(chips - 1)
    for d in range(1, chips):
        map_copy(d).wait()

    maps = [got[(chip - i + chips) % chips] for i in range(chips)]

    def tree(parts):
        if len(parts) == 1:
            return parts
        half = len(parts) // 2
        pairs = [then(parts[2 * i], parts[2 * i + 1]) for i in range(half)]
        return pairs

    level = maps
    levels = [maps]
    while len(level) > 1:
        level = tree(level)
        levels.append(level)
    mine[...] = level[0]

    def group_copy(d):
        return pltpu.make_async_remote_copy(
            src_ref=mine, dst_ref=groups.at[d],
            send_sem=send2.at[d], recv_sem=recv2.at[d],
            device_id=((group + d) % outer, me), device_id_type=mesh_id,
        )

    def first_copy(d):
        half = (slice(None), pl.ds(128, 128))
        return pltpu.make_async_remote_copy(
            src_ref=mine.at[half], dst_ref=groups.at[(d,) + half],
            send_sem=send2.at[d], recv_sem=recv2.at[d],
            device_id=((group + d) % outer, me), device_id_type=mesh_id,
        )

    for d in range(1, outer):

        @pl.when((group + d < outer) & (group > 0))
        def _():
            group_copy(d).start()

    @pl.when(group == 0)
    def _():
        for d in range(1, outer):
            first_copy(d).start()

    before = {}
    for i in range(1, chips):
        low = i & -i
        height = low.bit_length() - 1
        part = levels[height][(i - low) >> height]
        before[i] = part if i == low else then(before[i - low], part)
    left = wide(jnp.concatenate([before[i][:, :128] for i in range(1, chips)], 0))
    right = jnp.concatenate([before[i][:, 128:] for i in range(1, chips)], 0)

    for d in range(1, outer):

        @pl.when((group + d < outer) & (group > 0))
        def _():
            group_copy(d).wait_send()

        @pl.when(group - d > 0)
        def _():
            group_copy(d).wait_recv()

        @pl.when(group == d)
        def _():
            first_copy(d).wait_recv()

    @pl.when(group == 0)
    def _():
        for d in range(1, outer):
            first_copy(d).wait_send()

    start = jnp.where(group > 0, groups[group][:, 128:], 0.0)
    for g in range(1, outer - 1):
        pair = groups[(group - g + outer) % outer]
        moved = mul(pair[:, :128], start) + pair[:, 128:]
        start = jnp.where(g < group, moved, start)

    sh, sl = split(start)
    row = jnp.concatenate([sh, sl], 1)
    both = dot(left, jnp.concatenate([row, row], 0))
    ready[0] = start
    ready[pl.ds(1, chips - 1)] = (both[:, :128] + both[:, 128:] + right).reshape(chips - 1, 128, 128)

    def back_copy(d):
        to = (chip + d) % chips
        return pltpu.make_async_remote_copy(
            src_ref=ready.at[to], dst_ref=came.at[d],
            send_sem=send3.at[d], recv_sem=recv3.at[d],
            device_id=(group, to * 2 + core), device_id_type=mesh_id,
        )

    def side_copy(d):
        return pltpu.make_async_remote_copy(
            src_ref=aside.at[d], dst_ref=beside.at[d],
            send_sem=send4.at[d], recv_sem=recv4.at[d],
            device_id=(group, partner), device_id_type=mesh_id,
        )

    for d in range(1, chips):
        back_copy(d).start()

    def out(head, state):
        lanes = pl.ds(pl.multiple_of(head * 128, 128), 128)
        o_ref[:, lanes] = normed(c_buf[head], b_buf[head], state, g_ref[...])

    for d in range(chips):
        if d:
            back_copy(d).wait()
            enter = came[d]
        else:
            enter = ready[chip]
        pair = even_map[(chips - d) % chips]
        after = mul(pair[:, :128], enter) + pair[:, 128:]
        aside[d] = jnp.where(core == 0, after, enter)
        side_copy(d).start()
        far = (chip - d + chips) % chips * 2
        out(far + core, jnp.where(core == 0, enter, after))
        if d:
            side_copy(d - 1).wait()
            out((chip - d + 1 + chips) % chips * 2 + 1 - core, beside[d - 1])
    side_copy(chips - 1).wait()
    out((chip + 1) % chips * 2 + 1 - core, beside[chips - 1])


def whole(inner, outer, queries, keys, values, betas, log_decay, out_gain):
    length, width = queries.shape
    vmem = pl.BlockSpec(memory_space=pltpu.VMEM)
    dma = pltpu.SemaphoreType.DMA
    return pl.pallas_call(
        functools.partial(whole_kernel, inner, outer),
        in_specs=[vmem] * 6,
        out_specs=vmem,
        out_shape=jax.ShapeDtypeStruct((length, width), BF16),
        scratch_shapes=[
            *[pltpu.VMEM((inner // 2, 128, 256), F32)] * 6,
            pltpu.VMEM((outer, 128, 256), F32),
            pltpu.VMEM((128, 256), F32),
            *[pltpu.VMEM((inner // 2, 128, 128), F32)] * 4,
            *[pltpu.VMEM((inner, length, 128), F32)] * 2,
            pltpu.VMEM((2 * (length // BLOCK_LEN), inner, 128), F32),
            *[dma((inner // 2,))] * 4,
            *[dma((outer,))] * 2,
            *[dma((inner // 2,))] * 4,
        ],
        compiler_params=pltpu.CompilerParams(collective_id=0, has_side_effects=True),
        name="whole",
    )(queries, keys, values, betas, log_decay, out_gain.reshape(1, 128))


HIGHEST = lax.Precision.HIGHEST


def join(earlier, later):
    moved = jnp.einsum("hde,hef->hdf", later[..., :128], earlier, precision=HIGHEST)
    return jnp.concatenate([moved[..., :128], moved[..., 128:] + later[..., 128:]], -1)


def entering(pairs, axis, begin):
    gathered = lax.all_gather(pairs, axis)

    def one(hop, state):
        return join(state, lax.dynamic_index_in_dim(gathered, hop, 0, False))

    return lax.fori_loop(0, lax.axis_index(axis), one, begin)


def exchange_plain(pairs):
    eye = jnp.concatenate([jnp.eye(128, dtype=F32), jnp.zeros((128, 128), F32)], 1)
    begin = jnp.zeros_like(pairs) + eye
    before = entering(pairs, "inner", begin)
    through = join(before, pairs)
    last = lax.axis_index("inner") == lax.axis_size("inner") - 1
    total = lax.psum(jnp.where(last, through, 0.0), "inner")
    start = entering(total, "outer", begin)
    return join(start, before)[..., 128:]


def finish_kernel(c_ref, b_ref, e_ref, g_ref, o_ref):
    readout = mul(c_ref[0], e_ref[0]) + b_ref[0]
    mean_sq = jnp.mean(readout * readout, 1, keepdims=True)
    o_ref[...] = (readout * lax.rsqrt(mean_sq + 1e-05) * g_ref[...]).astype(BF16)


def finish(carried, base, state, out_gain):
    heads, length, _ = carried.shape
    return pl.pallas_call(
        finish_kernel,
        grid=(heads,),
        in_specs=[
            pl.BlockSpec((1, length, 128), lambda h: (h, 0, 0)),
            pl.BlockSpec((1, length, 128), lambda h: (h, 0, 0)),
            pl.BlockSpec((1, 128, 128), lambda h: (h, 0, 0)),
            pl.BlockSpec((1, 128), lambda h: (0, 0)),
        ],
        out_specs=pl.BlockSpec((length, 128), lambda h: (0, h)),
        out_shape=jax.ShapeDtypeStruct((length, heads * 128), BF16),
        name="finish",
    )(carried, base, state, out_gain.reshape(1, 128))


def per_device(inner, outer, queries, keys, values, betas, log_decay, out_gain):
    heads = betas.shape[1]
    if inner == heads:
        return whole(inner, outer, queries, keys, values, betas, log_decay, out_gain)
    pairs, carried, base = local_phase(queries, keys, values, betas, log_decay)
    return finish(carried, base, exchange_plain(pairs), out_gain)


def solution(mesh):
    both = ("outer", "inner")
    placed = (P(both, None), P(None, both, None), P(None, both, None), P(None, None, both), P(None, both), P())
    return jax.shard_map(
        functools.partial(per_device, mesh.shape["inner"], mesh.shape["outer"]),
        mesh=mesh,
        in_specs=placed,
        out_specs=P(both, None),
        check_vma=False,
    )
```
